32 devices in a mesh: batch: 16 (over z, x, core), seq: 2 (over y).
Axes of the slice: x: 2, y: 2, z: 4, core: 2. Of those that a mesh axis runs over, the one named last changes fastest.
Arguments:
- queries: bfloat16 [16, 256, 2048], P('batch', 'seq'), may hold values from -16 to 16
- key_states: bfloat16 [16, 256, 512], P('batch', 'seq'), may hold values from -6 to 6
- value_states: bfloat16 [16, 256, 512], P('batch', 'seq'), may hold values from -6 to 6
- lengths: int32 [16], P('batch'), may hold values from 32 to 256, as said below
- positives: int32 [16], P('batch'), may hold values from 0 to 15, each once
- query_emb: float32 [16, 1024], P('batch'), may hold values from -6 to 6
- projection: bfloat16 [2048, 1024], P('batch'), may hold values from -0.125 to 0.125
Outputs:
- loss_value: float32 [], replicated
- grad_query: float32 [16, 1024], P('batch')
- grad_proj: float32 [2048, 1024], P('batch')
- grad_values: bfloat16 [16, 256, 512], P('batch', 'seq')
The draws below stay inside these ranges and needn't reach their ends.
Inputs may be any that keep to these rules, and one draw needn't show every extreme that they name: `lengths`: every passage has at least 32 valid tokens, and some passage is full. `positives`: each passage is the positive of exactly one query.
All inputs are finite; a program needn't handle non-finite values.
Results may differ from the reference program's by a relative error of at most 0.012.
Values may be sent and summed in bfloat16 or wider, within the bound.
No kernel may reach another device: no remote copies, remote signals or barrier semaphores. Data moves between devices by JAX's collectives and lax.ppermute only.
A program may use at most 64 MiB of HBM per device.

```python
import math
import jax
import jax.numpy as jnp
from jax import lax

HEAD_DIM = 128
KV_HEADS = 4
EMB = 1024
GROUP = 4
FEAT = 2048
PAIRS = 16
PASS_LEN = 256


def draw_pair_states(key):
    folded = jax.random.fold_in(key, 7101)
    key_a, key_b = jax.random.split(folded)
    keys_f = jnp.clip(jax.random.normal(key_b, (PAIRS, PASS_LEN, KV_HEADS * HEAD_DIM), jnp.float32), -6.0, 6.0)
    query_f = jnp.clip(jax.random.normal(key_a, (PAIRS, PASS_LEN, FEAT), jnp.float32), -6.0, 6.0)
    spread = jnp.repeat(keys_f.reshape(PAIRS, PASS_LEN, KV_HEADS, HEAD_DIM), GROUP, axis=2).reshape(PAIRS, PASS_LEN, FEAT)
    places = jnp.arange(PASS_LEN, dtype=jnp.int32)
    first_span = PASS_LEN // 8
    target = places % first_span
    far_rows = (places >= first_span) & (places % 4 == 3)
    far_scale = 2.0
    far_copy = far_scale * jnp.take(spread, target, axis=1)
    query_f = jnp.where(far_rows[None, :, None], far_copy, query_f)
    return (query_f, keys_f)


def draw_queries(key, part):
    return draw_pair_states(key)[0].astype(jnp.bfloat16)


def draw_key_states(key, part):
    return draw_pair_states(key)[1].astype(jnp.bfloat16)


def draw_lengths(key, part):
    folded = jax.random.fold_in(key, 7303)
    first_key, second_key = jax.random.split(folded)
    drawn = jax.random.randint(first_key, (PAIRS,), PASS_LEN // 8, PASS_LEN + 1)
    chosen = jax.random.randint(second_key, (), 0, PAIRS)
    return jnp.where(jnp.arange(PAIRS) == chosen, PASS_LEN, drawn).astype(jnp.int32)


def levels(key, shape, shards, smallest, largest):
    level = 1.0
    for axis_at, shards_of in shards:
        draws = jax.random.uniform(jax.random.fold_in(jax.random.fold_in(key, 6), axis_at), (shards_of,), jnp.float32, smallest / len(shards), largest / len(shards))
        level = level * jnp.repeat(jnp.exp(draws), shape[axis_at] // shards_of).reshape((-1,) + (1,) * (len(shape) - 1 - axis_at))
    return level


def bell_draw(own_key, dims, deviation, most, cuts=(), kind=jnp.bfloat16):
    values = jax.random.normal(own_key, dims, jnp.float32) * deviation
    if len(cuts) > 0:
        values = levels(own_key, dims, cuts, -0.22, 0.18) * values
    return jnp.clip(values, min=-most, max=most).astype(kind)


def setup_inputs(seed: int = 0) -> dict:
    key_list = jax.random.split(jax.random.key(seed), 8)
    queries = draw_queries(jax.random.fold_in(key_list[7], 71), 0)
    key_states = draw_key_states(jax.random.fold_in(key_list[7], 71), 0)
    value_states = bell_draw(key_list[2], (PAIRS, PASS_LEN, KV_HEADS * HEAD_DIM), 1.0, 6.0, ((0, 16), (1, 2)))
    lengths = draw_lengths(jax.random.fold_in(key_list[7], 71), 0)
    positives = jax.random.permutation(key_list[4], PAIRS).astype(jnp.int32)
    query_emb = bell_draw(key_list[5], (PAIRS, EMB), 1.0, 6.0, ((0, 16),), jnp.float32)
    projection = bell_draw(key_list[6], (FEAT, EMB), FEAT ** -0.5, 0.125, ((0, 16),))
    return dict(queries=queries, key_states=key_states, value_states=value_states, lengths=lengths, positives=positives, query_emb=query_emb, projection=projection)


sharpness_divisor = 0.02
epsilon = 1e-06

def visible_mask(seq_len, length):
    positions = jnp.arange(seq_len, dtype=jnp.int32)
    return (positions[None, :] <= positions[:, None]) & (positions[None, :] < length)

def pool_weights(seq_len, length):
    positions = jnp.arange(seq_len, dtype=jnp.int32)
    return jnp.where(positions < length, jnp.float32(1.0), jnp.float32(0.0)) / length.astype(jnp.float32)

def passage_scores(query_row, key_row):
    seq_len = query_row.shape[0]
    query_grid = query_row.astype(jnp.float32).reshape(seq_len, KV_HEADS, GROUP, HEAD_DIM)
    key_grid = key_row.astype(jnp.float32).reshape(seq_len, KV_HEADS, HEAD_DIM)
    return jnp.einsum('sgrd,tgd->grst', query_grid, key_grid) / math.sqrt(HEAD_DIM)

def passage_forward(inputs):
    query_row, key_row, value_row, length = inputs
    seq_len = query_row.shape[0]
    scores = passage_scores(query_row, key_row)
    visible = visible_mask(seq_len, length)
    masked = jnp.where(visible, scores, jnp.float32(-1e+30))
    row_top = lax.optimization_barrier(jnp.max(masked, axis=-1))
    softmax_portions = jnp.where(visible, jnp.exp(masked - row_top[..., None]), jnp.float32(0.0))
    row_sum = lax.optimization_barrier(jnp.sum(softmax_portions, axis=-1))
    weights_low = softmax_portions.astype(jnp.bfloat16).astype(jnp.float32)
    value_grid = value_row.astype(jnp.float32).reshape(seq_len, KV_HEADS, HEAD_DIM)
    attended = jnp.einsum('grst,tgd->grsd', weights_low, value_grid) / row_sum[..., None]
    token_pool_weight = pool_weights(seq_len, length)
    pooled = jnp.einsum('s,grsd->grd', token_pool_weight, attended).reshape(KV_HEADS * GROUP * HEAD_DIM)
    return (pooled, row_top + jnp.log(row_sum))

def passage_backward(inputs):
    query_row, key_row, length, log_total, grad_pool = inputs
    seq_len = query_row.shape[0]
    scores = passage_scores(query_row, key_row)
    visible = visible_mask(seq_len, length)
    softmax_portions = jnp.exp(jnp.where(visible, scores - log_total[..., None], jnp.float32(-1e+30)))
    token_pool_weight = pool_weights(seq_len, length)
    column_total = jnp.einsum('mqnh,n->mqh', softmax_portions, token_pool_weight)
    gradient_table = grad_pool.reshape(KV_HEADS, GROUP, HEAD_DIM)
    gradient_row_block = jnp.einsum('lye,lyq->elq', column_total, gradient_table)
    return gradient_row_block.reshape(seq_len, KV_HEADS * HEAD_DIM).astype(jnp.bfloat16)

def reference(queries, key_states, value_states, lengths, positives, query_emb, projection):
    pooled, log_totals = lax.map(passage_forward, (queries, key_states, value_states, lengths))
    pooled_low = pooled.astype(jnp.bfloat16)
    embedding = jnp.dot(pooled_low, projection, preferred_element_type=jnp.float32)
    pass_norm = jnp.sqrt(lax.optimization_barrier(jnp.sum(embedding * embedding, axis=-1, keepdims=True)) + epsilon)
    document_direction = embedding / pass_norm
    query_norm = jnp.sqrt(lax.optimization_barrier(jnp.sum(query_emb * query_emb, axis=-1, keepdims=True)) + epsilon)
    question_direction = query_emb / query_norm
    cosine_score_matrix = jnp.dot(question_direction, document_direction.T, precision=lax.Precision.HIGHEST) / sharpness_divisor
    row_top = lax.optimization_barrier(jnp.max(cosine_score_matrix, axis=-1, keepdims=True))
    log_z = row_top + jnp.log(lax.optimization_barrier(jnp.sum(jnp.exp(cosine_score_matrix - row_top), axis=-1, keepdims=True)))
    pair_count = cosine_score_matrix.shape[0]
    onehot = (jnp.arange(pair_count, dtype=jnp.int32)[None, :] == positives[:, None]).astype(jnp.float32)
    loss_value = jnp.mean(log_z[:, 0] - lax.optimization_barrier(jnp.sum(onehot * cosine_score_matrix, axis=-1)))
    dscore_matrix = (jnp.exp(cosine_score_matrix - log_z) - onehot) / pair_count
    question_direction_adjoint = jnp.dot(dscore_matrix, document_direction, precision=lax.Precision.HIGHEST) / sharpness_divisor
    document_direction_adjoint = jnp.dot(dscore_matrix.T, question_direction, precision=lax.Precision.HIGHEST) / sharpness_divisor
    grad_query = (question_direction_adjoint - question_direction * lax.optimization_barrier(jnp.sum(question_direction * question_direction_adjoint, axis=-1, keepdims=True))) / query_norm
    dembedding = (document_direction_adjoint - document_direction * lax.optimization_barrier(jnp.sum(document_direction * document_direction_adjoint, axis=-1, keepdims=True))) / pass_norm
    grad_proj = jnp.dot(pooled_low.astype(jnp.float32).T, dembedding, precision=lax.Precision.HIGHEST)
    dpooled = jnp.dot(dembedding, projection.astype(jnp.float32).T, precision=lax.Precision.HIGHEST)
    grad_values = lax.map(passage_backward, (queries, key_states, lengths, log_totals, dpooled))
    return (loss_value, grad_query, grad_proj, grad_values)
```

```python
import math

import jax
import jax.numpy as jnp
from jax import lax
from jax.sharding import PartitionSpec as P

HEAD_DIM = 128
KV_HEADS = 4
GROUP = 4
Q_HEADS = KV_HEADS * GROUP
LANES = 128

sharpness_divisor = 0.02
epsilon = 1e-06

f32 = jnp.float32
bf16 = jnp.bfloat16
HIGHEST = lax.Precision.HIGHEST


def split_low(value):
    high = value.astype(bf16)
    return high, (value - high.astype(f32)).astype(bf16)


def per_device(queries, key_states, value_states, lengths, positives, query_emb, projection):
    tok = queries.shape[1]
    feat = queries.shape[2]
    rows, emb = projection.shape
    nb = lax.axis_size("batch")
    ns = lax.axis_size("seq")
    cols = emb // nb
    fold = LANES // cols
    seq_rank = lax.axis_index("seq")
    batch_rank = lax.axis_index("batch")
    length = lengths[0]
    inv_root = 1.0 / math.sqrt(HEAD_DIM)

    if ns == 2:
        past_keys = lax.ppermute(key_states[0], "seq", [(0, 1)])
        past_values = lax.ppermute(value_states[0], "seq", [(0, 1)])
    else:
        past_keys = lax.all_gather(key_states[0], "seq", axis=0, tiled=True)
        past_values = lax.all_gather(value_states[0], "seq", axis=0, tiled=True)

    part = rows // fold
    folded = projection.reshape(fold, part, nb, cols).transpose(2, 1, 0, 3).reshape(nb, part, LANES)
    query_high, query_low = split_low(query_emb.reshape(emb // LANES, LANES))
    place = jnp.broadcast_to(positives[0].astype(bf16), (8, LANES))
    shared = jnp.concatenate([query_high, query_low, place], axis=0)
    first_out = jnp.concatenate(
        [folded, jnp.broadcast_to(shared[None], (nb,) + shared.shape)], axis=1
    )
    first_in = lax.all_to_all(first_out, "batch", 0, 0, tiled=True)
    proj_cols = (
        first_in[:, :part].reshape(nb, part, fold, cols).transpose(0, 2, 1, 3).reshape(feat, cols)
    )
    q_rows = emb // LANES
    query_all = first_in[:, part : part + q_rows].astype(f32) + first_in[
        :, part + q_rows : part + 2 * q_rows
    ].astype(f32)
    query_all = query_all.reshape(nb, emb)
    positive_all = first_in[:, part + 2 * q_rows, 0].astype(jnp.int32)

    past = past_keys.shape[0]
    query_grid = queries[0].reshape(tok, KV_HEADS, GROUP, HEAD_DIM)
    keys_now = jnp.concatenate([past_keys, key_states[0]], axis=0)
    values_now = jnp.concatenate([past_values, value_states[0]], axis=0)
    start = seq_rank * tok
    s_pos = start + jnp.arange(tok, dtype=jnp.int32)
    index = jnp.arange(past + tok, dtype=jnp.int32)
    t_pos = jnp.where(index < past, index, index - past + start)
    counted = (index >= past) | (index < start)
    visible = (t_pos[None, :] <= s_pos[:, None]) & (t_pos < length)[None, :] & counted[None, :]
    scores = (
        jnp.einsum(
            "sgrd,tgd->grst",
            query_grid,
            keys_now.reshape(past + tok, KV_HEADS, HEAD_DIM),
            preferred_element_type=f32,
        )
        * inv_root
    )
    masked = jnp.where(visible, scores, f32(-1e30))
    row_top = jnp.max(masked, axis=-1)
    portions = jnp.exp(masked - row_top[..., None])
    row_sum = jnp.sum(portions, axis=-1)
    token_weight = jnp.where(s_pos < length, 1.0, 0.0).astype(f32) / length.astype(f32)
    colsum = jnp.sum(portions * (token_weight / row_sum)[..., None], axis=2)
    pooled_part = jnp.einsum(
        "grt,tgd->grd",
        colsum,
        values_now.reshape(past + tok, KV_HEADS, HEAD_DIM).astype(f32),
        precision=HIGHEST,
    ).reshape(Q_HEADS, HEAD_DIM)
    colsum = colsum.reshape(Q_HEADS, past + tok)
    if ns == 2:
        returned = lax.ppermute(colsum[:, :past], "seq", [(1, 0)])
    else:
        returned = lax.psum_scatter(colsum[:, :past], "seq", scatter_dimension=1, tiled=True)
    colsum_here = colsum[:, past:] + returned

    second_out = jnp.broadcast_to(pooled_part.astype(bf16)[None], (nb * ns, Q_HEADS, HEAD_DIM))
    second_in = lax.all_to_all(second_out, ("batch", "seq"), 0, 0, tiled=True)
    pooled_parts = second_in.reshape(nb * ns, feat)

    query_norm = jnp.sqrt(jnp.sum(query_all * query_all, axis=-1, keepdims=True) + epsilon)
    query_unit = query_all / query_norm
    query_proj = lax.dot_general(
        query_unit, projection.astype(f32), (((1,), (1,)), ((), ())), precision=HIGHEST
    )

    emb_cols = jnp.dot(pooled_parts, proj_cols, preferred_element_type=f32)
    emb_cols = jnp.sum(emb_cols.reshape(nb, ns, cols), axis=1)
    back_part = lax.dot_general(
        emb_cols, proj_cols.astype(f32), (((1,), (1,)), ((), ())), precision=HIGHEST
    )

    emb_high, emb_low = split_low(emb_cols)
    emb_block = jnp.concatenate([emb_high, emb_low], axis=1).reshape(-1, LANES)
    common = jnp.concatenate([emb_block, query_proj.astype(bf16).reshape(-1, LANES)], axis=0)
    third_out = jnp.concatenate(
        [
            jnp.broadcast_to(common[None], (nb,) + common.shape),
            back_part.astype(bf16).reshape(nb, feat // LANES, LANES),
        ],
        axis=1,
    )
    third_in = lax.all_to_all(third_out, "batch", 0, 0, tiled=True)
    e_rows = emb_block.shape[0]
    p_rows = common.shape[0]
    emb_in = third_in[:, :e_rows].reshape(nb, nb, 2, cols).astype(f32)
    embedding = jnp.sum(emb_in, axis=2).transpose(1, 0, 2).reshape(nb, emb)
    query_proj_all = (
        third_in[:, e_rows:p_rows].reshape(nb, nb, rows).transpose(1, 0, 2).reshape(nb, feat)
    ).astype(f32)
    back_here = jnp.sum(third_in[:, p_rows:].astype(f32), axis=0).reshape(feat)

    pass_norm = jnp.sqrt(jnp.sum(embedding * embedding, axis=-1, keepdims=True) + epsilon)
    pass_unit = embedding / pass_norm
    logits = (
        lax.dot_general(query_unit, pass_unit, (((1,), (1,)), ((), ())), precision=HIGHEST)
        / sharpness_divisor
    )
    top = jnp.max(logits, axis=-1, keepdims=True)
    log_z = top + jnp.log(jnp.sum(jnp.exp(logits - top), axis=-1, keepdims=True))
    onehot = (jnp.arange(nb, dtype=jnp.int32)[None, :] == positive_all[:, None]).astype(f32)
    loss_value = jnp.sum(log_z[:, 0] - jnp.sum(onehot * logits, axis=-1)) / nb
    dlogits = (jnp.exp(logits - log_z) - onehot) / nb
    dlogits_mine = lax.dynamic_slice_in_dim(dlogits, batch_rank, 1, 0)
    unit_mine = lax.dynamic_slice_in_dim(query_unit, batch_rank, 1, 0)
    norm_mine = lax.dynamic_slice_in_dim(query_norm, batch_rank, 1, 0)
    dquery = jnp.dot(dlogits_mine, pass_unit, precision=HIGHEST) / sharpness_divisor
    grad_query = (dquery - unit_mine * jnp.sum(unit_mine * dquery, axis=-1, keepdims=True)) / norm_mine
    dpass = (
        lax.dot_general(dlogits, query_unit, (((0,), (0,)), ((), ())), precision=HIGHEST)
        / sharpness_divisor
    )
    radial = jnp.sum(pass_unit * dpass, axis=-1, keepdims=True)
    dembedding = (dpass - pass_unit * radial) / pass_norm
    pooled_rows = lax.dynamic_slice_in_dim(pooled_parts, batch_rank * rows, rows, 1).astype(f32)
    pooled_rows = jnp.sum(pooled_rows.reshape(nb, ns, rows), axis=1)
    grad_proj = lax.dot_general(
        pooled_rows, dembedding, (((0,), (0,)), ((), ())), precision=HIGHEST
    )

    dlogits_col = lax.dynamic_slice_in_dim(dlogits, batch_rank, 1, 1)
    norm_b = lax.dynamic_slice_in_dim(pass_norm, batch_rank, 1, 0)[0, 0]
    radial_b = lax.dynamic_slice_in_dim(radial, batch_rank, 1, 0)[0, 0]
    dpooled = (
        jnp.sum(dlogits_col * query_proj_all, axis=0) / sharpness_divisor
        - radial_b * back_here / norm_b
    ) / norm_b
    grad_values = jnp.einsum(
        "grt,grd->tgd",
        colsum_here.reshape(KV_HEADS, GROUP, tok),
        dpooled.reshape(KV_HEADS, GROUP, HEAD_DIM),
        precision=HIGHEST,
    ).reshape(1, tok, KV_HEADS * HEAD_DIM)
    return (loss_value, grad_query, grad_proj, grad_values.astype(bf16))


def solution(mesh):
    placed = (
        P("batch", "seq", None),
        P("batch", "seq", None),
        P("batch", "seq", None),
        P("batch"),
        P("batch"),
        P("batch", None),
        P("batch", None),
    )
    return jax.shard_map(
        per_device,
        mesh=mesh,
        in_specs=placed,
        out_specs=(P(), P("batch", None), P("batch", None), P("batch", "seq", None)),
        check_vma=False,
    )
```

```python
import math

import jax
import jax.numpy as jnp
from jax import lax
from jax.experimental import pallas as pl
from jax.experimental.pallas import tpu as pltpu
from jax.sharding import PartitionSpec as P

HEAD_DIM = 128
KV_HEADS = 4
GROUP = 4
Q_HEADS = KV_HEADS * GROUP
LANES = 128

sharpness_divisor = 0.02
epsilon = 1e-06

f32 = jnp.float32
bf16 = jnp.bfloat16
HIGHEST = lax.Precision.HIGHEST


def split_low(value):
    high = value.astype(bf16)
    return high, (value - high.astype(f32)).astype(bf16)


def per_device_any(queries, key_states, value_states, lengths, positives, query_emb, projection):
    tok = queries.shape[1]
    feat = queries.shape[2]
    rows, emb = projection.shape
    nb = lax.axis_size("batch")
    ns = lax.axis_size("seq")
    cols = emb // nb
    fold = LANES // cols
    seq_rank = lax.axis_index("seq")
    batch_rank = lax.axis_index("batch")
    length = lengths[0]
    inv_root = 1.0 / math.sqrt(HEAD_DIM)

    if ns == 2:
        past_keys = lax.ppermute(key_states[0], "seq", [(0, 1)])
        past_values = lax.ppermute(value_states[0], "seq", [(0, 1)])
    else:
        past_keys = lax.all_gather(key_states[0], "seq", axis=0, tiled=True)
        past_values = lax.all_gather(value_states[0], "seq", axis=0, tiled=True)

    part = rows // fold
    folded = projection.reshape(fold, part, nb, cols).transpose(2, 1, 0, 3).reshape(nb, part, LANES)
    query_high, query_low = split_low(query_emb.reshape(emb // LANES, LANES))
    place = jnp.broadcast_to(positives[0].astype(bf16), (8, LANES))
    shared = jnp.concatenate([query_high, query_low, place], axis=0)
    first_out = jnp.concatenate(
        [folded, jnp.broadcast_to(shared[None], (nb,) + shared.shape)], axis=1
    )
    first_in = lax.all_to_all(first_out, "batch", 0, 0, tiled=True)
    proj_cols = (
        first_in[:, :part].reshape(nb, part, fold, cols).transpose(0, 2, 1, 3).reshape(feat, cols)
    )
    q_rows = emb // LANES
    query_all = first_in[:, part : part + q_rows].astype(f32) + first_in[
        :, part + q_rows : part + 2 * q_rows
    ].astype(f32)
    query_all = query_all.reshape(nb, emb)
    positive_all = first_in[:, part + 2 * q_rows, 0].astype(jnp.int32)

    past = past_keys.shape[0]
    query_grid = queries[0].reshape(tok, KV_HEADS, GROUP, HEAD_DIM)
    keys_now = jnp.concatenate([past_keys, key_states[0]], axis=0)
    values_now = jnp.concatenate([past_values, value_states[0]], axis=0)
    start = seq_rank * tok
    s_pos = start + jnp.arange(tok, dtype=jnp.int32)
    index = jnp.arange(past + tok, dtype=jnp.int32)
    t_pos = jnp.where(index < past, index, index - past + start)
    counted = (index >= past) | (index < start)
    visible = (t_pos[None, :] <= s_pos[:, None]) & (t_pos < length)[None, :] & counted[None, :]
    scores = (
        jnp.einsum(
            "sgrd,tgd->grst",
            query_grid,
            keys_now.reshape(past + tok, KV_HEADS, HEAD_DIM),
            preferred_element_type=f32,
        )
        * inv_root
    )
    masked = jnp.where(visible, scores, f32(-1e30))
    row_top = jnp.max(masked, axis=-1)
    portions = jnp.exp(masked - row_top[..., None])
    row_sum = jnp.sum(portions, axis=-1)
    token_weight = jnp.where(s_pos < length, 1.0, 0.0).astype(f32) / length.astype(f32)
    colsum = jnp.sum(portions * (token_weight / row_sum)[..., None], axis=2)
    pooled_part = jnp.einsum(
        "grt,tgd->grd",
        colsum,
        values_now.reshape(past + tok, KV_HEADS, HEAD_DIM).astype(f32),
        precision=HIGHEST,
    ).reshape(Q_HEADS, HEAD_DIM)
    colsum = colsum.reshape(Q_HEADS, past + tok)
    if ns == 2:
        returned = lax.ppermute(colsum[:, :past], "seq", [(1, 0)])
    else:
        returned = lax.psum_scatter(colsum[:, :past], "seq", scatter_dimension=1, tiled=True)
    colsum_here = colsum[:, past:] + returned

    second_out = jnp.broadcast_to(pooled_part.astype(bf16)[None], (nb * ns, Q_HEADS, HEAD_DIM))
    second_in = lax.all_to_all(second_out, ("batch", "seq"), 0, 0, tiled=True)
    pooled_parts = second_in.reshape(nb * ns, feat)

    query_norm = jnp.sqrt(jnp.sum(query_all * query_all, axis=-1, keepdims=True) + epsilon)
    query_unit = query_all / query_norm
    query_proj = lax.dot_general(
        query_unit, projection.astype(f32), (((1,), (1,)), ((), ())), precision=HIGHEST
    )

    emb_cols = jnp.dot(pooled_parts, proj_cols, preferred_element_type=f32)
    emb_cols = jnp.sum(emb_cols.reshape(nb, ns, cols), axis=1)
    back_part = lax.dot_general(
        emb_cols, proj_cols.astype(f32), (((1,), (1,)), ((), ())), precision=HIGHEST
    )

    emb_high, emb_low = split_low(emb_cols)
    emb_block = jnp.concatenate([emb_high, emb_low], axis=1).reshape(-1, LANES)
    common = jnp.concatenate([emb_block, query_proj.astype(bf16).reshape(-1, LANES)], axis=0)
    third_out = jnp.concatenate(
        [
            jnp.broadcast_to(common[None], (nb,) + common.shape),
            back_part.astype(bf16).reshape(nb, feat // LANES, LANES),
        ],
        axis=1,
    )
    third_in = lax.all_to_all(third_out, "batch", 0, 0, tiled=True)
    e_rows = emb_block.shape[0]
    p_rows = common.shape[0]
    emb_in = third_in[:, :e_rows].reshape(nb, nb, 2, cols).astype(f32)
    embedding = jnp.sum(emb_in, axis=2).transpose(1, 0, 2).reshape(nb, emb)
    query_proj_all = (
        third_in[:, e_rows:p_rows].reshape(nb, nb, rows).transpose(1, 0, 2).reshape(nb, feat)
    ).astype(f32)
    back_here = jnp.sum(third_in[:, p_rows:].astype(f32), axis=0).reshape(feat)

    pass_norm = jnp.sqrt(jnp.sum(embedding * embedding, axis=-1, keepdims=True) + epsilon)
    pass_unit = embedding / pass_norm
    logits = (
        lax.dot_general(query_unit, pass_unit, (((1,), (1,)), ((), ())), precision=HIGHEST)
        / sharpness_divisor
    )
    top = jnp.max(logits, axis=-1, keepdims=True)
    log_z = top + jnp.log(jnp.sum(jnp.exp(logits - top), axis=-1, keepdims=True))
    onehot = (jnp.arange(nb, dtype=jnp.int32)[None, :] == positive_all[:, None]).astype(f32)
    loss_value = jnp.sum(log_z[:, 0] - jnp.sum(onehot * logits, axis=-1)) / nb
    dlogits = (jnp.exp(logits - log_z) - onehot) / nb
    dlogits_mine = lax.dynamic_slice_in_dim(dlogits, batch_rank, 1, 0)
    unit_mine = lax.dynamic_slice_in_dim(query_unit, batch_rank, 1, 0)
    norm_mine = lax.dynamic_slice_in_dim(query_norm, batch_rank, 1, 0)
    dquery = jnp.dot(dlogits_mine, pass_unit, precision=HIGHEST) / sharpness_divisor
    grad_query = (dquery - unit_mine * jnp.sum(unit_mine * dquery, axis=-1, keepdims=True)) / norm_mine
    dpass = (
        lax.dot_general(dlogits, query_unit, (((0,), (0,)), ((), ())), precision=HIGHEST)
        / sharpness_divisor
    )
    radial = jnp.sum(pass_unit * dpass, axis=-1, keepdims=True)
    dembedding = (dpass - pass_unit * radial) / pass_norm
    pooled_rows = lax.dynamic_slice_in_dim(pooled_parts, batch_rank * rows, rows, 1).astype(f32)
    pooled_rows = jnp.sum(pooled_rows.reshape(nb, ns, rows), axis=1)
    grad_proj = lax.dot_general(
        pooled_rows, dembedding, (((0,), (0,)), ((), ())), precision=HIGHEST
    )

    dlogits_col = lax.dynamic_slice_in_dim(dlogits, batch_rank, 1, 1)
    norm_b = lax.dynamic_slice_in_dim(pass_norm, batch_rank, 1, 0)[0, 0]
    radial_b = lax.dynamic_slice_in_dim(radial, batch_rank, 1, 0)[0, 0]
    dpooled = (
        jnp.sum(dlogits_col * query_proj_all, axis=0) / sharpness_divisor
        - radial_b * back_here / norm_b
    ) / norm_b
    grad_values = jnp.einsum(
        "grt,grd->tgd",
        colsum_here.reshape(KV_HEADS, GROUP, tok),
        dpooled.reshape(KV_HEADS, GROUP, HEAD_DIM),
        precision=HIGHEST,
    ).reshape(1, tok, KV_HEADS * HEAD_DIM)
    return (loss_value, grad_query, grad_proj, grad_values.astype(bf16))


def dot_t(left, right, precision=None):
    return lax.dot_general(
        left, right, (((1,), (1,)), ((), ())), precision=precision, preferred_element_type=f32
    )


def dot_0(left, right):
    return lax.dot_general(left, right, (((0,), (0,)), ((), ())), preferred_element_type=f32)


def lane_of(shape):
    return lax.broadcasted_iota(jnp.int32, shape, 1)


def swap(value):
    return pltpu.roll(value, LANES // 2, 1)


def pack_kernel(positive_ref, proj_ref, query_ref, out_ref, line_ref):
    nb, width, _ = out_ref.shape
    rows, emb = proj_ref.shape
    part = rows // 2
    q_rows = emb // LANES
    low = lane_of((part, LANES)) < LANES // 2
    for tile in range(emb // LANES):
        block = proj_ref[:, tile * LANES : (tile + 1) * LANES].astype(f32)
        upper, lower = block[:part], block[part:]
        out_ref[2 * tile, :part] = jnp.where(low, upper, swap(lower)).astype(bf16)
        out_ref[2 * tile + 1, :part] = jnp.where(low, swap(upper), lower).astype(bf16)
    for row in range(q_rows):
        line_ref[row : row + 1, :] = query_ref[:, row * LANES : (row + 1) * LANES]
    lines = line_ref[...]
    high = lines.astype(bf16).astype(f32)
    place = jnp.full((8, LANES), positive_ref[0], jnp.int32).astype(f32)
    shared = jnp.concatenate([high, lines - high, place], axis=0).astype(bf16)
    for dest in range(nb):
        out_ref[dest, part:] = shared


def attend_kernel(
    length_ref,
    query_ref,
    key_ref,
    value_ref,
    past_key_ref,
    past_value_ref,
    out_ref,
    own_ref,
    past_ref,
):
    tok = query_ref.shape[1]
    past = past_key_ref.shape[0]
    start = lax.axis_index("seq") * tok
    length = length_ref[0]
    scale = 1.0 / math.sqrt(HEAD_DIM)
    row = lax.broadcasted_iota(jnp.int32, (tok, tok), 0)
    col = lax.broadcasted_iota(jnp.int32, (tok, tok), 1)
    own_seen = (col <= row) & (col + start < length)
    past_seen = lax.broadcasted_iota(jnp.int32, (tok, past), 1) < jnp.minimum(start, length)
    s_pos = lax.broadcasted_iota(jnp.int32, (tok, 1), 0) + start
    weight = jnp.where(s_pos < length, 1.0, 0.0).astype(f32) / length.astype(f32)
    head_row = lax.broadcasted_iota(jnp.int32, (Q_HEADS, tok), 0)
    own_sum = jnp.zeros((Q_HEADS, tok), f32)
    past_sum = jnp.zeros((Q_HEADS, past), f32)
    for head in range(Q_HEADS):
        group = head // GROUP
        q = query_ref[0, :, head * HEAD_DIM : (head + 1) * HEAD_DIM]
        at = slice(group * HEAD_DIM, (group + 1) * HEAD_DIM)
        own = jnp.where(own_seen, dot_t(q, key_ref[0, :, at]) * scale, -1e30)
        old = jnp.where(past_seen, dot_t(q, past_key_ref[:, at]) * scale, -1e30)
        top = jnp.max(jnp.maximum(own, old), axis=1, keepdims=True)
        own = jnp.exp(own - top)
        old = jnp.exp(old - top)
        share = weight / jnp.sum(own + old, axis=1, keepdims=True)
        own_sum = jnp.where(head_row == head, jnp.sum(own * share, axis=0, keepdims=True), own_sum)
        past_sum = jnp.where(head_row == head, jnp.sum(old * share, axis=0, keepdims=True), past_sum)
    own_ref[...] = own_sum
    past_ref[...] = past_sum
    total = jnp.zeros((2 * Q_HEADS, KV_HEADS * HEAD_DIM), f32)
    for sums, values in ((own_sum, value_ref[0]), (past_sum, past_value_ref[...])):
        high = sums.astype(bf16)
        lower = (sums - high.astype(f32)).astype(bf16)
        total += jnp.dot(
            jnp.concatenate([high, lower], axis=0), values, preferred_element_type=f32
        )
    both = total[:Q_HEADS] + total[Q_HEADS:]
    group_row = lax.broadcasted_iota(jnp.int32, (Q_HEADS, HEAD_DIM), 0) // GROUP
    pooled = jnp.zeros((Q_HEADS, HEAD_DIM), f32)
    for group in range(KV_HEADS):
        pooled = jnp.where(
            group_row == group, both[:, group * HEAD_DIM : (group + 1) * HEAD_DIM], pooled
        )
    pooled = pooled.astype(bf16)
    for dest in range(out_ref.shape[0]):
        out_ref[dest] = pooled


def query_kernel(first_ref, proj_ref, unit_ref, norm_ref, place_ref, back_ref, line_ref, mark_ref):
    nb = first_ref.shape[0]
    rows, emb = proj_ref.shape
    part = rows // 2
    q_rows = emb // LANES
    for src in range(nb):
        block = first_ref[src, part : part + 2 * q_rows].astype(f32)
        line_ref[src * q_rows : (src + 1) * q_rows] = block[:q_rows] + block[q_rows:]
        mark_ref[src * 8 : (src + 1) * 8] = first_ref[src, part + 2 * q_rows :].astype(f32)
    query = jnp.concatenate(
        [line_ref[pl.ds(row, nb, stride=q_rows), :] for row in range(q_rows)], axis=1
    )
    place_ref[...] = mark_ref[pl.ds(0, nb, stride=8), :]
    norm = jnp.sqrt(jnp.sum(query * query, axis=1, keepdims=True) + epsilon)
    unit = query / norm
    unit_ref[...] = unit
    norm_ref[...] = jnp.broadcast_to(norm, norm_ref.shape)
    high = unit.astype(bf16)
    lower = (unit - high.astype(f32)).astype(bf16)
    both = dot_t(jnp.concatenate([high, lower], axis=0), proj_ref[...])
    back_ref[...] = (both[:nb] + both[nb:]).astype(bf16)


def middle_kernel(second_ref, first_ref, back_ref, out_ref, rows_ref, flat_ref, fold_ref):
    nb = out_ref.shape[0]
    ns = second_ref.shape[0] // nb
    part = HEAD_DIM // 2
    for src in range(nb * ns):
        flat_ref[src * Q_HEADS : (src + 1) * Q_HEADS] = second_ref[src].astype(f32)

    def head_of(head):
        return [
            flat_ref[pl.ds(head + Q_HEADS * s, nb, stride=ns * Q_HEADS), :] for s in range(ns)
        ]

    rank = lax.axis_index("batch")
    for s in range(ns):
        rows_ref[s * nb : (s + 1) * nb] = flat_ref[
            pl.ds(rank + Q_HEADS * s, nb, stride=ns * Q_HEADS), :
        ]
    m = nb * ns
    low = lane_of((m, LANES)) < LANES // 2
    upper, lower = [], []
    for pair in range(Q_HEADS // 2):
        even = jnp.concatenate(head_of(2 * pair), axis=0)
        odd = jnp.concatenate(head_of(2 * pair + 1), axis=0)
        upper.append(jnp.where(low, even, swap(odd)))
        lower.append(jnp.where(low, swap(even), odd))
    left = jnp.concatenate(
        [jnp.concatenate(upper, axis=1), jnp.concatenate(lower, axis=1)], axis=0
    ).astype(bf16)
    cols = jnp.concatenate([first_ref[src, :part] for src in range(nb)], axis=0)
    prod = jnp.dot(left, cols, preferred_element_type=f32)
    both = jnp.where(low, prod[:m], prod[m:])
    both = both + swap(both)
    emb = both[:nb]
    for s in range(1, ns):
        emb = emb + both[s * nb : (s + 1) * nb]
    low = low[:nb]
    high = emb.astype(bf16).astype(f32)
    rest = emb - high
    block = jnp.where(low, high, rest).astype(bf16)
    zero = jnp.zeros_like(emb)
    left = jnp.concatenate(
        [
            jnp.where(low, high, zero),
            jnp.where(low, zero, high),
            jnp.where(low, rest, zero),
            jnp.where(low, zero, rest),
        ],
        axis=0,
    ).astype(bf16)
    back = dot_t(left, cols)
    back = back[: 2 * nb] + back[2 * nb :]
    for pair in range(Q_HEADS // 2):
        upper = back[:nb, pair * LANES : (pair + 1) * LANES]
        lower = back[nb:, pair * LANES : (pair + 1) * LANES]
        fold_ref[pl.ds(2 * pair, nb, stride=Q_HEADS), :] = jnp.where(low, upper, swap(lower))
        fold_ref[pl.ds(2 * pair + 1, nb, stride=Q_HEADS), :] = jnp.where(low, swap(upper), lower)
    common = back_ref[...]
    for dest in range(nb):
        out_ref[dest, :nb] = block
        out_ref[dest, nb : 2 * nb] = common
        out_ref[dest, 2 * nb :] = fold_ref[dest * Q_HEADS : (dest + 1) * Q_HEADS].astype(bf16)


def final_kernel(
    third_ref,
    rows_ref,
    unit_ref,
    norm_ref,
    place_ref,
    own_ref,
    other_ref,
    loss_ref,
    gquery_ref,
    gproj_ref,
    gvalue_ref,
):
    nb, emb_width = unit_ref.shape
    rank = lax.axis_index("batch")
    low = lane_of((nb, LANES)) < LANES // 2
    tiles = []
    for pair in range(nb // 2):
        even = third_ref[2 * pair, :nb].astype(f32)
        odd = third_ref[2 * pair + 1, :nb].astype(f32)
        tiles.append(jnp.where(low, even + swap(even), odd + swap(odd)))
    emb = jnp.concatenate(tiles, axis=1)
    norm = jnp.sqrt(jnp.sum(emb * emb, axis=1, keepdims=True) + epsilon)
    unit = emb / norm
    query = unit_ref[...]
    logits = dot_t(query, unit, HIGHEST) / sharpness_divisor
    top = jnp.max(logits, axis=1, keepdims=True)
    log_z = top + jnp.log(jnp.sum(jnp.exp(logits - top), axis=1, keepdims=True))
    row = lax.broadcasted_iota(jnp.int32, (nb, nb), 0)
    col = lax.broadcasted_iota(jnp.int32, (nb, nb), 1)
    hot = jnp.where(col == place_ref[:, :1].astype(jnp.int32), 1.0, 0.0).astype(f32)
    terms = log_z - jnp.sum(hot * logits, axis=1, keepdims=True)
    loss_ref[...] = jnp.sum(terms, axis=0, keepdims=True) / nb
    dlogits = (jnp.exp(logits - log_z) - hot) / nb
    eye = jnp.where(row == col, 1.0, 0.0).astype(f32)
    turned = dot_t(eye, dlogits, HIGHEST)
    dpass = jnp.dot(turned, query, precision=HIGHEST, preferred_element_type=f32) / sharpness_divisor
    radial = jnp.sum(unit * dpass, axis=1, keepdims=True)
    demb = (dpass - unit * radial) / norm

    mine = col == rank
    by_pass = jnp.sum(jnp.where(mine, turned, 0.0), axis=1, keepdims=True)
    by_query = jnp.sum(jnp.where(mine, dlogits, 0.0), axis=1, keepdims=True)
    dquery = jnp.sum(by_pass * unit, axis=0, keepdims=True) / sharpness_divisor
    unit_here = unit_ref[pl.ds(rank, 1), :]
    norm_here = norm_ref[pl.ds(rank, 1), :][:, :1]
    gquery_ref[...] = (
        dquery - unit_here * jnp.sum(unit_here * dquery, axis=1, keepdims=True)
    ) / norm_here

    high = demb.astype(bf16)
    lower = (demb - high.astype(f32)).astype(bf16)
    ns = rows_ref.shape[0] // nb
    left = rows_ref[...].astype(bf16)
    gproj_ref[...] = dot_0(
        jnp.concatenate([left, left], axis=0),
        jnp.concatenate([high] * ns + [lower] * ns, axis=0),
    )

    mine_row = lax.broadcasted_iota(jnp.int32, (nb, 1), 0) == rank
    norm_b = jnp.sum(jnp.where(mine_row, norm, 0.0), axis=0, keepdims=True)
    radial_b = jnp.sum(jnp.where(mine_row, radial, 0.0), axis=0, keepdims=True)
    back = third_ref[0, 2 * nb :].astype(f32)
    for src in range(1, nb):
        back = back + third_ref[src, 2 * nb :].astype(f32)
    head_row = lax.broadcasted_iota(jnp.int32, (Q_HEADS, HEAD_DIM), 0)
    direct = jnp.zeros((Q_HEADS, HEAD_DIM), f32)
    for src in range(nb):
        line = jnp.sum(third_ref[src, nb : 2 * nb].astype(f32) * by_query, axis=0, keepdims=True)
        direct = jnp.where(head_row == src, line, direct)
    dpool = (direct / sharpness_divisor - back * (radial_b / norm_b)) / norm_b
    group_row = head_row // GROUP
    spread = jnp.concatenate(
        [jnp.where(group_row == group, dpool, 0.0) for group in range(KV_HEADS)], axis=1
    )
    sums = own_ref[...] + other_ref[...]
    sums_high = sums.astype(bf16)
    sums_low = (sums - sums_high.astype(f32)).astype(bf16)
    high = spread.astype(bf16)
    lower = (spread - high.astype(f32)).astype(bf16)
    gvalue_ref[0] = dot_0(
        jnp.concatenate([sums_high, sums_high, sums_low], axis=0),
        jnp.concatenate([high, lower, high], axis=0),
    ).astype(bf16)


def vmem(shape, dtype):
    return pltpu.VMEM(shape, dtype)


SMEM_SPEC = pl.BlockSpec(memory_space=pltpu.SMEM)
VMEM_SPEC = pl.BlockSpec(memory_space=pltpu.VMEM)


def call(kernel, name, in_specs, outs, scratch):
    shapes = tuple(jax.ShapeDtypeStruct(shape, dtype) for shape, dtype in outs)
    return pl.pallas_call(
        kernel,
        name=name,
        in_specs=in_specs,
        out_specs=tuple(VMEM_SPEC for _ in outs),
        out_shape=shapes,
        scratch_shapes=scratch,
    )


def per_device_paired(queries, key_states, value_states, lengths, positives, query_emb, projection):
    tok = queries.shape[1]
    rows, emb = projection.shape
    nb = lax.axis_size("batch")
    ns = lax.axis_size("seq")
    part = rows // 2
    width = part + 2 * (emb // LANES) + 8
    kv = KV_HEADS * HEAD_DIM
    past_keys = lax.ppermute(key_states[0], "seq", [(0, 1)])
    past_values = lax.ppermute(value_states[0], "seq", [(0, 1)])
    (first_out,) = call(
        pack_kernel,
        "pack",
        [SMEM_SPEC, VMEM_SPEC, VMEM_SPEC],
        [((nb, width, LANES), bf16)],
        [vmem((emb // LANES, LANES), f32)],
    )(positives, projection, query_emb)
    first_in = lax.all_to_all(first_out, "batch", 0, 0, tiled=True)
    second_out, own_sum, past_sum = call(
        attend_kernel,
        "attend",
        [SMEM_SPEC] + [VMEM_SPEC] * 5,
        [
            ((nb * ns, Q_HEADS, HEAD_DIM), bf16),
            ((Q_HEADS, tok), f32),
            ((Q_HEADS, tok), f32),
        ],
        [],
    )(lengths, queries, key_states, value_states, past_keys, past_values)
    other_sum = lax.ppermute(past_sum, "seq", [(1, 0)])
    second_in = lax.all_to_all(second_out, ("batch", "seq"), 0, 0, tiled=True)
    unit, norm, place, query_back = call(
        query_kernel,
        "query",
        [VMEM_SPEC, VMEM_SPEC],
        [((nb, emb), f32), ((nb, LANES), f32), ((nb, LANES), f32), ((nb, rows), bf16)],
        [vmem((nb * emb // LANES, LANES), f32), vmem((nb * 8, LANES), f32)],
    )(first_in, projection)
    third_out, pooled_rows = call(
        middle_kernel,
        "middle",
        [VMEM_SPEC, VMEM_SPEC, VMEM_SPEC],
        [((nb, 2 * nb + Q_HEADS, LANES), bf16), ((nb * ns, rows), f32)],
        [vmem((nb * ns * Q_HEADS, LANES), f32), vmem((nb * Q_HEADS, LANES), f32)],
    )(second_in, first_in, query_back)
    third_in = lax.all_to_all(third_out, "batch", 0, 0, tiled=True)
    loss, grad_query, grad_proj, grad_values = call(
        final_kernel,
        "final",
        [VMEM_SPEC] * 7,
        [((1, 1), f32), ((1, emb), f32), ((rows, emb), f32), ((1, tok, kv), bf16)],
        [],
    )(third_in, pooled_rows, unit, norm, place, own_sum, other_sum)
    return (loss[0, 0], grad_query, grad_proj, grad_values)


def per_device(queries, key_states, value_states, lengths, positives, query_emb, projection):
    rows, emb = projection.shape
    nb = lax.axis_size("batch")
    ns = lax.axis_size("seq")
    paired = ns == 2 and rows == HEAD_DIM and 2 * emb == nb * LANES and nb == Q_HEADS
    run = per_device_paired if paired else per_device_any
    return run(queries, key_states, value_states, lengths, positives, query_emb, projection)


def solution(mesh):
    placed = (
        P("batch", "seq", None),
        P("batch", "seq", None),
        P("batch", "seq", None),
        P("batch"),
        P("batch"),
        P("batch", None),
        P("batch", None),
    )
    return jax.shard_map(
        per_device,
        mesh=mesh,
        in_specs=placed,
        out_specs=(P(), P("batch", None), P("batch", None), P("batch", "seq", None)),
        check_vma=False,
    )
```
